32 devices in a mesh: wide: 8 (over z, y), narrow: 4 (over x, core).
Axes of the slice: x: 2, y: 2, z: 4, core: 2. Of those that a mesh axis runs over, the one named last changes fastest.
Arguments:
- prior_lt: float32 [4096, 6144], P('narrow', 'wide'), may hold values from -2 to 2
- prior_d: float32 [4096], P('narrow'), may hold values from -4 to 4
- prior_e: float32 [4096], P('narrow'), may hold values from -4 to 4
- prior_pairs: int32 [4096], P('narrow'), may hold values from 0 to 1, as said below
- pivots: int32 [2, 256], replicated, may hold values from 0 to 6143, as said below
- a_first: float32 [256, 6144], P('narrow', 'wide'), may hold values from -6 to 6
- a_second: float32 [256, 6144], P('narrow', 'wide'), may hold values from -6 to 6
- inv_d: float32 [2, 256], P(None, 'narrow'), may hold values from -4 to 4
- inv_e: float32 [2, 256], P(None, 'narrow'), may hold values from -4 to 4
- panel_pairs: int32 [2, 256], P(None, 'narrow'), may hold values from 0 to 1, as said below
Outputs:
- l_first: float32 [256, 6144], P('narrow', 'wide')
- l_second: float32 [256, 6144], P('narrow', 'wide')
The draws below stay inside these ranges and needn't reach their ends.
Inputs may be any that keep to these rules, and one draw needn't show every extreme that they name: `pivots`: all 512 pivot rows are distinct; at most 128 of them lie in one tile of 768 consecutive rows, and some tile holds exactly 128. `prior_pairs`: 1 only at even positions; a 1 at position k joins k and k + 1 into a 2 x 2 pivot block. `panel_pairs`: 1 only at even positions along the last dimension; a 1 at position k joins k and k + 1 into a 2 x 2 pivot block.
All inputs are finite; a program needn't handle non-finite values.
Results may differ from the reference program's by a relative error of at most 0.000098.
Values sent between devices are 32-bit elements; how exact they have to be, the bound alone decides.
A program may use at most 64 MiB of HBM per device.

```python
import jax
import jax.numpy as jnp
from jax import lax

ROWS = 768
K = 4096
P_SIZE = 256
N = 6144
CAP = 128
N_WIDE = 8


def draw_pivots(key, part):
    key_order = jax.random.fold_in(key, 11)
    key_full = jax.random.fold_in(key, 12)
    key_rows = jax.random.fold_in(key, 13)
    key_mix = jax.random.fold_in(key, 14)
    total_slots = N_WIDE * CAP
    order = jax.random.permutation(key_order, total_slots)
    full_tile = jax.random.randint(key_full, (), 0, N_WIDE)
    owner = order // CAP
    score = jnp.where(owner == full_tile, 0, total_slots) + jnp.arange(total_slots)
    picked = order[jnp.argsort(score)[:2 * P_SIZE]]
    tile = picked // CAP
    within = picked % CAP
    row_order = jax.random.permutation(key_rows, ROWS)
    offset = (row_order[within] + tile * 7) % ROWS
    rows_all = tile * ROWS + offset
    rows_all = jax.random.permutation(key_mix, rows_all)
    return rows_all.reshape(2, P_SIZE).astype(jnp.int32)


def draw_prior_pairs(key, part):
    bits = jax.random.randint(jax.random.fold_in(key, 21), (K // 2,), 0, 2)
    return jnp.stack([bits, jnp.zeros_like(bits)], 1).reshape(K).astype(jnp.int32)


def draw_panel_pairs(key, part):
    bits = jax.random.randint(jax.random.fold_in(key, 31), (2, P_SIZE // 2), 0, 2)
    return jnp.stack([bits, jnp.zeros_like(bits)], 2).reshape(2, P_SIZE).astype(jnp.int32)


def shard_levels(rng, extent, cuts, smallest, high):
    factor_of = 1.0
    for dim, shards_of in cuts:
        heights = jax.random.uniform(jax.random.fold_in(jax.random.fold_in(rng, 6), dim), (shards_of,), jnp.float32, smallest / len(cuts), high / len(cuts))
        factor_of = factor_of * jnp.repeat(jnp.exp(heights), extent[dim] // shards_of).reshape((-1,) + (1,) * (len(extent) - 1 - dim))
    return factor_of


def noise(rng, extent, deviation, most, split=(), kind=jnp.bfloat16):
    entries = jax.random.normal(rng, extent, jnp.float32) * deviation
    if len(split) > 0:
        entries = shard_levels(rng, extent, split, -0.22, 0.18) * entries
    return jnp.clip(entries, min=-most, max=most).astype(kind)


def setup_inputs(seed: int = 0) -> dict:
    arg_keys = jax.random.split(jax.random.key(seed), 11)
    return {
        "prior_lt": noise(arg_keys[0], (K, N), (1.0 / K ** 0.25), 2.0, ((0, 4), (1, 8)), jnp.float32),
        "prior_d": noise(arg_keys[1], (K,), 1.0, 4.0, ((0, 4),), jnp.float32),
        "prior_e": noise(arg_keys[2], (K,), 0.5, 4.0, ((0, 4),), jnp.float32),
        "prior_pairs": draw_prior_pairs(jax.random.fold_in(arg_keys[10], 71), 0),
        "pivots": draw_pivots(jax.random.fold_in(arg_keys[10], 71), 0),
        "a_first": noise(arg_keys[5], (P_SIZE, N), 1.0, 6.0, ((0, 4), (1, 8)), jnp.float32),
        "a_second": noise(arg_keys[6], (P_SIZE, N), 1.0, 6.0, ((0, 4), (1, 8)), jnp.float32),
        "inv_d": noise(arg_keys[7], (2, P_SIZE), 0.3, 4.0, ((1, 4),), jnp.float32),
        "inv_e": noise(arg_keys[8], (2, P_SIZE), 0.3, 4.0, ((1, 4),), jnp.float32),
        "panel_pairs": draw_panel_pairs(jax.random.fold_in(arg_keys[10], 71), 0),
    }


def couple(block, diag, off, pairs):
    joined = off * pairs.astype(jnp.float32)
    zero_row = jnp.zeros_like(block[:1])
    after = jnp.concatenate([block[1:], zero_row], 0)
    before = jnp.concatenate([zero_row, block[:-1]], 0)
    lower = jnp.concatenate([jnp.zeros_like(joined[:1]), joined[:-1]], 0)
    return diag[:, None] * block + joined[:, None] * after + lower[:, None] * before


def reference(prior_lt, prior_d, prior_e, prior_pairs, pivots, a_first, a_second, inv_d, inv_e, panel_pairs):
    flat = pivots.reshape(-1)
    chosen = jnp.take(prior_lt, flat, axis=1)
    coupled = couple(chosen, prior_d, prior_e, prior_pairs)
    update = lax.dot_general(coupled, prior_lt, (((0,), (0,)), ((), ())), precision=lax.Precision.HIGHEST)
    width = a_first.shape[0]
    w_first = a_first - update[:width]
    l_first = couple(w_first, inv_d[0], inv_e[0], panel_pairs[0])
    crossed = jnp.take(l_first, pivots[1], axis=1)
    correction = lax.dot_general(crossed, w_first, (((0,), (0,)), ((), ())), precision=lax.Precision.HIGHEST)
    w_second = a_second - update[width:] - correction
    l_second = couple(w_second, inv_d[1], inv_e[1], panel_pairs[1])
    return l_first, l_second
```

```python
import functools

import jax
import jax.numpy as jnp
from jax import lax
from jax.experimental import pallas as pl
from jax.experimental.pallas import tpu as pltpu
from jax.sharding import PartitionSpec as P

F32 = jnp.float32
BF16 = jnp.bfloat16
NN = (((1,), (0,)), ((), ()))
NT = (((1,), (1,)), ((), ()))


def dot(a, b, dims=NN):
    return lax.dot_general(a, b, dims, preferred_element_type=F32)


def halves(x):
    hi = x.astype(BF16)
    return hi, (x - hi.astype(F32)).astype(BF16)


def dot3(ahi, alo, bhi, blo, dims=NN):
    return dot(ahi, bhi, dims) + (dot(ahi, blo, dims) + dot(alo, bhi, dims))


def couple(block, diag, after, before, axis):
    size = block.shape[axis]
    return (
        diag * block
        + after * pltpu.roll(block, size - 1, axis)
        + before * pltpu.roll(block, 1, axis)
    )


def kernel(
    n_wide, n_narrow, cap,
    prior, kcol, krow, loc, loc_a, slot, slot_a, a_one, a_two, inv,
    l_one, l_two,
    got, got_a, dhi, dlo, chi, clo, ehi, elo, part, part2, from_core, from_core2, mid, mid2,
    from_x, from_x2, wall, turned,
    s_right, s_left, s_pair, recv, sa_right, sa_left, sa_pair, recv_a,
    s1, r1, s2, r2, s3, r3, s4, r4, s5, r5, s6, r6,
):
    k_local, tile = prior.shape
    blocks = a_one.shape[0]
    panel = blocks * n_narrow
    line = n_wide // 2
    chips = n_narrow // 2
    w = lax.axis_index("wide")
    n = lax.axis_index("narrow")
    a, b = w // 2, w % 2
    x, core = n // 2, n % 2
    pair = a * 2 + (1 - b)
    has_left, has_right = a > 0, a < line - 1

    barrier = pltpu.get_barrier_semaphore()

    def greet(**where):
        pl.semaphore_signal(barrier, inc=1, device_id=where, device_id_type=pl.DeviceIdType.MESH)

    def nar(cx, cc):
        return {"wide": w, "narrow": cx * 2 + cc}

    greet(wide=pair, narrow=n)

    @pl.when(has_left)
    def _():
        greet(wide=w - 2, narrow=n)

    @pl.when(has_right)
    def _():
        greet(wide=w + 2, narrow=n)

    greet(wide=w, narrow=x * 2 + (1 - core))
    for step in range(1, chips):
        greet(wide=w, narrow=lax.rem(x + step, chips) * 2 + core)

    pick = (loc[...] == lax.broadcasted_iota(jnp.int32, (cap, tile), 1)).astype(F32).astype(BF16)
    piece = 256
    for k in range(0, k_local, piece):
        hi, lo = halves(prior[k:k + piece, :])
        got[w, :, k:k + piece] = dot(pick, hi, NT) + dot(pick, lo, NT)
    wide_a = got_a.shape[2]
    pick_a = (loc_a[...] == lax.broadcasted_iota(jnp.int32, (wide_a, tile), 1)).astype(F32).astype(BF16)
    hi, lo = halves(a_one[...])
    got_a[w] = dot(hi, pick_a, NT) + dot(lo, pick_a, NT)

    ends = (a == 0).astype(jnp.int32) + (a == line - 1).astype(jnp.int32)
    pl.semaphore_wait(barrier, chips + 3 - ends)

    def move(buf, item, send, sem_at, rsem, to):
        return pltpu.make_async_remote_copy(
            src_ref=buf.at[item], dst_ref=buf.at[item], send_sem=send.at[sem_at], recv_sem=rsem.at[item],
            device_id={"wide": to, "narrow": n}, device_id_type=pl.DeviceIdType.MESH,
        )

    def both(item, which, to):
        at = item // 2
        return (
            move(got, item, (s_right, s_left, s_pair)[which], at, recv, to),
            move(got_a, item, (sa_right, sa_left, sa_pair)[which], at, recv_a, to),
        )

    def go(item, which, to):
        for c in both(item, which, to):
            c.start()

    def landed(item):
        for c in both(item, 0, pair):
            c.wait_recv()

    @pl.when(has_right)
    def _():
        go(w, 0, w + 2)

    @pl.when(has_left)
    def _():
        go(w, 1, w - 2)

    go(w, 2, pair)

    for k in range(0, k_local, 128):
        sl = slice(k, k + 128)
        m = couple(prior[sl, :], kcol[sl, 0:1], kcol[sl, 1:2], kcol[sl, 2:3], 0)
        hi, lo = halves(m)
        dhi[sl, :] = hi
        dlo[sl, :] = lo

    def relay(t, _):
        @pl.when(a - t >= 0)
        def _():
            item = w - 2 * t
            landed(item)
            go(item, 2, pair)

            @pl.when(has_right)
            def _():
                go(item, 0, w + 2)

        @pl.when(a + t < line)
        def _():
            item = w + 2 * t
            landed(item)
            go(item, 2, pair)

            @pl.when(has_left)
            def _():
                go(item, 1, w - 2)

        return 0

    lax.fori_loop(1, line, relay, 0)

    def from_pair(t, _):
        landed(t * 2 + (1 - b))
        return 0

    lax.fori_loop(0, line, from_pair, 0)

    slots = n_wide * cap
    put = (slot[...] == lax.broadcasted_iota(jnp.int32, (2 * panel, slots), 1)).astype(F32).astype(BF16)
    for k in range(0, k_local, piece):
        sl = slice(k, k + piece)
        hi, lo = halves(got[:, :, sl].reshape(slots, piece))
        ch, cl = dot(put, hi), dot(put, lo)
        chi[:, sl] = ch.astype(BF16)
        clo[:, sl] = cl.astype(BF16)
        c2 = ch[panel:] + cl[panel:]
        eh, el = halves(couple(c2, krow[0:1, sl], krow[1:2, sl], krow[2:3, sl], 1))
        ehi[:, sl] = eh
        elo[:, sl] = el

    def fold(v):
        return v.reshape(n_narrow, blocks, v.shape[-1])

    part[:, :, tile:] = fold(dot3(chi[:panel, :], clo[:panel, :], ehi[...], elo[...], NT))
    for c in range(0, tile, 256):
        cs = slice(c, c + 256)
        part[:, :, cs] = fold(dot3(chi[:panel, :], clo[:panel, :], dhi[:, cs], dlo[:, cs]))

    def rc(src, dst, ss, rs, to):
        return pltpu.make_async_remote_copy(
            src_ref=src, dst_ref=dst, send_sem=ss, recv_sem=rs, device_id=to, device_id_type=pl.DeviceIdType.MESH,
        )

    def chip_at(s):
        return lax.rem(x + 1 + s, chips)

    def core_swap(src, dst, ss, rs):
        return [
            rc(src.at[chip_at(s) * 2 + (1 - core)], dst.at[s], ss.at[s], rs.at[s], nar(x, 1 - core))
            for s in range(chips)
        ]

    swap1 = core_swap(part, from_core, s1, r1)
    for c in swap1:
        c.start()
    for c in range(0, tile, 256):
        cs = slice(c, c + 256)
        part2[:, :, cs] = fold(dot3(chi[panel:, :], clo[panel:, :], dhi[:, cs], dlo[:, cs]))
    swap2 = core_swap(part2, from_core2, s2, r2)
    for c in swap2:
        c.start()

    def across(swap, src, held, middle, dst, ss, rs):
        out = []
        for s in range(chips - 1):
            swap[s].wait_recv()
            middle[s] = src[chip_at(s) * 2 + core] + held[s]
            c = rc(middle.at[s], dst.at[s], ss.at[s], rs.at[s], nar(chip_at(s), core))
            c.start()
            out.append(c)
        swap[chips - 1].wait_recv()
        return out

    def total(sent, src, held, dst):
        v = src[n] + held[chips - 1]
        for s, c in enumerate(sent):
            c.wait_recv()
            v = v + dst[s]
        return v

    sent1 = across(swap1, part, from_core, mid, from_x, s3, r3)

    def gather_a(i, acc):
        hi, lo = halves(got_a[i])
        p = (slot_a[...] - i * wide_a == lax.broadcasted_iota(jnp.int32, (wide_a, panel), 0)).astype(F32).astype(BF16)
        return acc + (dot(hi, p) + dot(lo, p))

    aq = lax.fori_loop(0, n_wide, gather_a, jnp.zeros((blocks, panel), F32))
    sent2 = across(swap2, part2, from_core2, mid2, from_x2, s4, r4)

    upd = total(sent1, part, from_core, from_x)
    w_one = a_one[...] - upd[:, :tile]
    wall[n, :, :tile] = w_one
    crossed = couple(aq - upd[:, tile:], inv[:, 0:1], inv[:, 1:2], inv[:, 2:3], 0)
    wall[n, :, tile:] = crossed

    spread = [rc(wall.at[n], wall.at[n], s5.at[s], r5.at[n], nar(chip_at(s), core)) for s in range(chips - 1)]
    for c in spread:
        c.start()
    twin = [rc(wall.at[n], wall.at[n], s6.at[0], r6.at[n], nar(x, 1 - core))]
    twin[0].start()
    l_one[...] = couple(w_one, inv[:, 0:1], inv[:, 1:2], inv[:, 2:3], 0)
    w_two = a_two[...] - total(sent2, part2, from_core2, from_x2)

    for s in range(chips - 1):
        item = chip_at(s) * 2 + core
        rc(wall.at[item], wall.at[item], s5.at[s], r5.at[item], nar(x, 1 - core)).wait_recv()
        c = rc(wall.at[item], wall.at[item], s6.at[s + 1], r6.at[item], nar(x, 1 - core))
        c.start()
        twin.append(c)
    for s in range(chips):
        item = chip_at(s) * 2 + (1 - core)
        rc(wall.at[item], wall.at[item], s6.at[s], r6.at[item], nar(x, 1 - core)).wait_recv()

    turned[...] = jnp.transpose(wall[:, :, tile:].reshape(panel, panel))
    ph, plo = halves(turned[pl.ds(pl.multiple_of(n * blocks, blocks), blocks), :])
    wh, wl = halves(wall[:, :, :tile].reshape(panel, tile))
    w_two = w_two - dot3(ph, plo, wh, wl)
    l_two[...] = couple(w_two, inv[:, 3:4], inv[:, 4:5], inv[:, 5:6], 0)

    for c in swap1 + swap2 + sent1 + sent2 + spread + twin:
        c.wait_send()

    def drain(t, _):
        item = t * 2 + b
        for c in both(item, 2, pair):
            c.wait_send()

        @pl.when((t <= a) & has_right)
        def _():
            for c in both(item, 0, pair):
                c.wait_send()

        @pl.when((t >= a) & has_left)
        def _():
            for c in both(item, 1, pair):
                c.wait_send()

        return 0

    lax.fori_loop(0, line, drain, 0)


def coefficients(diag, off, pairs, axis):
    joined = off * pairs.astype(F32)
    lower = jnp.concatenate([jnp.zeros_like(joined[:1]), joined[:-1]], 0)
    return [diag, joined, lower]


def shards(
    n_wide, n_narrow,
    prior_lt, prior_d, prior_e, prior_pairs, pivots, a_first, a_second, inv_d, inv_e, panel_pairs,
):
    k_local, tile = prior_lt.shape
    blocks = a_first.shape[0]
    panel = blocks * n_narrow
    cap = max(4 * panel // n_wide, 2)
    wide_a = -(-cap // 128) * 128
    line, chips = n_wide // 2, n_narrow // 2
    here = lax.axis_index("wide")
    flat = pivots.reshape(-1)
    owner = flat // tile
    order = jnp.arange(2 * panel)
    same = (owner[:, None] == owner[None, :]) & (order[:, None] > order[None, :])
    rank = jnp.sum(same.astype(jnp.int32), axis=1)
    hit = (owner[None, :] == here) & (rank[None, :] == jnp.arange(wide_a)[:, None])
    loc = jnp.sum(jnp.where(hit, (flat - here * tile + 1)[None, :], 0), axis=1) - 1
    slot = owner * cap + rank
    slot_a = (owner * wide_a + rank)[panel:]
    parts = coefficients(prior_d, prior_e, prior_pairs, 0)
    kcol, krow = jnp.stack(parts, 1), jnp.stack(parts, 0)
    inv = jnp.stack(
        coefficients(inv_d[0], inv_e[0], panel_pairs[0], 0) + coefficients(inv_d[1], inv_e[1], panel_pairs[1], 0), 1
    )
    dma = pltpu.SemaphoreType.DMA
    vm = pltpu.VMEM
    ext = tile + panel
    out = jax.ShapeDtypeStruct((blocks, tile), F32)
    return pl.pallas_call(
        functools.partial(kernel, n_wide, n_narrow, cap),
        out_shape=(out, out),
        in_specs=[pl.BlockSpec(memory_space=vm)] * 10,
        out_specs=(pl.BlockSpec(memory_space=vm),) * 2,
        scratch_shapes=[
            vm((n_wide, cap, k_local), F32),
            vm((n_wide, blocks, wide_a), F32),
            vm((k_local, tile), BF16),
            vm((k_local, tile), BF16),
            vm((2 * panel, k_local), BF16),
            vm((2 * panel, k_local), BF16),
            vm((panel, k_local), BF16),
            vm((panel, k_local), BF16),
            vm((n_narrow, blocks, ext), F32),
            vm((n_narrow, blocks, tile), F32),
            vm((chips, blocks, ext), F32),
            vm((chips, blocks, tile), F32),
            vm((chips, blocks, ext), F32),
            vm((chips, blocks, tile), F32),
            vm((chips, blocks, ext), F32),
            vm((chips, blocks, tile), F32),
            vm((n_narrow, blocks, ext), F32),
            vm((panel, panel), F32),
            dma((line,)), dma((line,)), dma((line,)), dma((n_wide,)),
            dma((line,)), dma((line,)), dma((line,)), dma((n_wide,)),
            dma((chips,)), dma((chips,)), dma((chips,)), dma((chips,)),
            dma((chips,)), dma((chips,)), dma((chips,)), dma((chips,)),
            dma((chips,)), dma((n_narrow,)), dma((chips,)), dma((n_narrow,)),
        ],
        compiler_params=pltpu.CompilerParams(
            collective_id=0, has_side_effects=True, vmem_limit_bytes=60 * 1024 * 1024
        ),
    )(
        prior_lt, kcol, krow, loc[:cap, None], loc[:, None], slot[:, None], slot_a[None, :],
        a_first, a_second, inv,
    )


def solution(mesh):
    in_specs = (
        P("narrow", "wide"),
        P("narrow"),
        P("narrow"),
        P("narrow"),
        P(),
        P("narrow", "wide"),
        P("narrow", "wide"),
        P(None, "narrow"),
        P(None, "narrow"),
        P(None, "narrow"),
    )
    out_specs = (P("narrow", "wide"), P("narrow", "wide"))
    body = functools.partial(shards, mesh.shape["wide"], mesh.shape["narrow"])
    return jax.shard_map(body, mesh=mesh, in_specs=in_specs, out_specs=out_specs, check_vma=False)
```

```python
import functools

import jax
import jax.numpy as jnp
from jax import lax
from jax.experimental import pallas as pl
from jax.experimental.pallas import tpu as pltpu
from jax.sharding import PartitionSpec as P

F32 = jnp.float32
BF16 = jnp.bfloat16
NN = (((1,), (0,)), ((), ()))
NT = (((1,), (1,)), ((), ()))


def dot(a, b, dims=NN):
    return lax.dot_general(a, b, dims, preferred_element_type=F32)


def halves(x):
    hi = x.astype(BF16)
    return hi, (x - hi.astype(F32)).astype(BF16)


def dot3(ahi, alo, bhi, blo, dims=NN):
    return dot(ahi, bhi, dims) + (dot(ahi, blo, dims) + dot(alo, bhi, dims))


def couple(block, diag, joined, axis):
    size = block.shape[axis]
    return diag * block + joined * pltpu.roll(block, size - 1, axis) + pltpu.roll(joined * block, 1, axis)


def count(shape, axis):
    return lax.broadcasted_iota(jnp.int32, shape, axis).astype(F32)


def column(row):
    size = row.shape[1]
    step = min(size, 128)
    eye = count((step, step), 0) == count((step, step), 1)
    return jnp.concatenate(
        [jnp.sum(jnp.where(eye, row[:, i:i + step], 0.0), axis=1, keepdims=True) for i in range(0, size, step)], 0
    )


def onehot(mask):
    return jnp.where(mask, 1.0, 0.0).astype(BF16)


def kernel(
    n_wide, n_narrow, cap, pieces,
    prior_hbm, diag, off, pairs, pivots, a_one, a_two, inv_d, inv_e, panel_pairs,
    l_one, l_two,
    prior, packed, inbox, dense, got_a, put, coef, dhi, dlo, part, part2, from_core, from_core2, mid, mid2,
    from_x, from_x2, wall, turned,
    s_load, s_post, r_post,
    s_right, s_left, s_pair, recv, sa_right, sa_left, sa_pair, recv_a,
    s1, r1, s2, r2, s3, r3, s4, r4, s5, r5, s6, r6,
):
    k_local, tile = prior.shape
    blocks = a_one.shape[0]
    panel = blocks * n_narrow
    kk = k_local // pieces
    line = n_wide // 2
    held = pieces // 2
    chips = n_narrow // 2
    wide_a = got_a.shape[2]
    w = lax.axis_index("wide")
    n = lax.axis_index("narrow")
    a, b = w // 2, w % 2
    x, core = n // 2, n % 2
    pair = a * 2 + (1 - b)
    has_left, has_right = a > 0, a < line - 1
    mesh_ids = pl.DeviceIdType.MESH

    loads = [
        pltpu.make_async_copy(prior_hbm.at[pl.ds(q * kk, kk)], prior.at[pl.ds(q * kk, kk)], s_load.at[q])
        for q in range(pieces)
    ]
    for c in loads:
        c.start()

    barrier = pltpu.get_barrier_semaphore()

    def greet(to, which):
        pl.semaphore_signal(barrier, inc=1, device_id={"wide": to, "narrow": which}, device_id_type=mesh_ids)

    def greet_wide(i, _):
        greet(lax.rem(w + i, n_wide), n)
        return 0

    lax.fori_loop(1, n_wide, greet_wide, 0)

    def nar(cx, cc):
        return {"wide": w, "narrow": cx * 2 + cc}

    greet(w, x * 2 + (1 - core))
    for step in range(1, chips):
        greet(w, lax.rem(x + step, chips) * 2 + core)

    flat = jnp.concatenate([pivots[0:1, :], pivots[1:2, :]], 1).astype(F32)
    owner = jnp.floor((flat + 0.5) * (1.0 / tile))
    square = (2 * panel, 2 * panel)
    same = (column(owner) == owner) & (count(square, 0) < count(square, 1))
    rank = jnp.sum(jnp.where(same, 1.0, 0.0), axis=0, keepdims=True)
    here = w.astype(F32)
    hit = (owner == here) & (rank == count((wide_a, 2 * panel), 0))
    loc = jnp.sum(jnp.where(hit, flat - here * tile + 1.0, 0.0), axis=1, keepdims=True) - 1.0
    pick_a = onehot(loc == count((wide_a, tile), 1))
    pick = pick_a[:cap]

    pl.semaphore_wait(barrier, n_wide - 1 + chips)

    def post(q):
        return pltpu.make_async_remote_copy(
            src_ref=packed.at[q], dst_ref=inbox.at[w], send_sem=s_post.at[q], recv_sem=r_post.at[w],
            device_id={"wide": q, "narrow": n}, device_id_type=mesh_ids,
        )

    for q in range(pieces):
        loads[q].wait()
        hi, lo = halves(prior[q * kk:(q + 1) * kk, :])
        packed[q] = dot(pick, hi, NT) + dot(pick, lo, NT)

        @pl.when(w != q)
        def _():
            post(q).start()

    def move(buf, item, send, sem_at, rsem, to):
        return pltpu.make_async_remote_copy(
            src_ref=buf.at[item], dst_ref=buf.at[item], send_sem=send.at[sem_at], recv_sem=rsem.at[item],
            device_id={"wide": to, "narrow": n}, device_id_type=mesh_ids,
        )

    def piece_to(item, which, to):
        return move(dense, item, (s_right, s_left, s_pair)[which], item // 2, recv, to)

    def a_to(item, which, to):
        return move(got_a, item, (sa_right, sa_left, sa_pair)[which], item // 2, recv_a, to)

    def send_own(make):
        @pl.when(has_right)
        def _():
            make(w, 0, w + 2).start()

        @pl.when(has_left)
        def _():
            make(w, 1, w - 2).start()

        make(w, 2, pair).start()

    hi, lo = halves(a_one[...])
    got_a[w] = dot(hi, pick_a, NT) + dot(lo, pick_a, NT)
    send_own(a_to)

    slots = n_wide * cap
    put[...] = onehot(column(owner * cap + rank) == count((2 * panel, slots), 1))
    joined = off[...] * pairs[...].astype(F32)
    for q in range(pieces):
        sl = slice(q * kk, (q + 1) * kk)
        coef[q, 0:1, :] = diag[:, sl]
        coef[q, 1:2, :] = joined[:, sl]

    @pl.when(w < pieces)
    def _():
        inbox[w] = packed[w]

        def arrived(j, _):
            @pl.when(j != w)
            def _():
                pltpu.make_async_remote_copy(
                    src_ref=packed.at[0], dst_ref=inbox.at[j], send_sem=s_post.at[0], recv_sem=r_post.at[j],
                    device_id={"wide": pair, "narrow": n}, device_id_type=mesh_ids,
                ).wait_recv()

            return 0

        lax.fori_loop(0, n_wide, arrived, 0)
        hi, lo = halves(inbox[...].reshape(slots, kk))
        dense[w] = dot(put[...], hi) + dot(put[...], lo)
        send_own(piece_to)

    for q in range(pieces):
        sl = slice(q * kk, (q + 1) * kk)
        m = couple(prior[sl, :], column(diag[:, sl]), column(joined[:, sl]), 0)
        hi, lo = halves(m)
        dhi[sl, :] = hi
        dlo[sl, :] = lo
    part[...] = jnp.zeros_like(part)
    part2[...] = jnp.zeros_like(part2)

    inv_j = inv_e[...] * panel_pairs[...].astype(F32)
    inv = [(column(inv_d[i:i + 1, :]), column(inv_j[i:i + 1, :])) for i in range(2)]

    def fold(v):
        return v.reshape(n_narrow, blocks, v.shape[-1])

    def add_pair(p):
        c = [dense[2 * p + i] for i in range(2)]
        e = [
            halves(couple(c[i][panel:], coef[2 * p + i, 0:1, :], coef[2 * p + i, 1:2, :], 1)) for i in range(2)
        ]
        c = [halves(v) for v in c]
        ch, cl = (jnp.concatenate([c[0][i], c[1][i]], 1) for i in range(2))
        eh, el = (jnp.concatenate([e[0][i], e[1][i]], 1) for i in range(2))
        rows = pl.ds(pl.multiple_of(p * 2 * kk, 2 * kk), 2 * kk)
        part[:, :, tile:] += fold(dot3(ch[:panel], cl[:panel], eh, el, NT))
        for j in range(0, tile, 256):
            cs = slice(j, j + 256)
            ph, pq = dhi[rows, cs], dlo[rows, cs]
            part[:, :, cs] += fold(dot3(ch[:panel], cl[:panel], ph, pq))
            part2[:, :, cs] += fold(dot3(ch[panel:], cl[panel:], ph, pq))

    def relay_item(make, item, ahead, which, to):
        make(item, 0, pair).wait_recv()
        make(item, 2, pair).start()

        @pl.when(ahead)
        def _():
            make(item, which, to).start()

    def step(t, _):
        for make, size in ((a_to, line), (piece_to, held)):
            @pl.when((t < line) & (a - t >= 0) & (a - t < size))
            def _():
                relay_item(make, w - 2 * t, has_right, 0, w + 2)

            @pl.when((t < line) & (a + t < size))
            def _():
                relay_item(make, w + 2 * t, has_left, 1, w - 2)

        def pair_at(p):
            piece_to(2 * p + (1 - b), 0, pair).wait_recv()
            add_pair(p)

        @pl.when((a - t + 1 >= 0) & (a - t + 1 < held))
        def _():
            pair_at(a - t + 1)

        @pl.when((t > 1) & (a + t - 1 < held))
        def _():
            pair_at(a + t - 1)

        return 0

    lax.fori_loop(1, line + 1, step, 0)

    def rc(src, dst, ss, rs, to):
        return pltpu.make_async_remote_copy(
            src_ref=src, dst_ref=dst, send_sem=ss, recv_sem=rs, device_id=to, device_id_type=pl.DeviceIdType.MESH,
        )

    def chip_at(s):
        return lax.rem(x + 1 + s, chips)

    def core_swap(src, dst, ss, rs):
        return [
            rc(src.at[chip_at(s) * 2 + (1 - core)], dst.at[s], ss.at[s], rs.at[s], nar(x, 1 - core))
            for s in range(chips)
        ]

    swap1 = core_swap(part, from_core, s1, r1)
    for c in swap1:
        c.start()
    swap2 = core_swap(part2, from_core2, s2, r2)
    for c in swap2:
        c.start()

    def across(swap, src, partner, middle, dst, ss, rs):
        out = []
        for s in range(chips - 1):
            swap[s].wait_recv()
            middle[s] = src[chip_at(s) * 2 + core] + partner[s]
            c = rc(middle.at[s], dst.at[s], ss.at[s], rs.at[s], nar(chip_at(s), core))
            c.start()
            out.append(c)
        swap[chips - 1].wait_recv()
        return out

    def total(sent, src, partner, dst):
        v = src[n] + partner[chips - 1]
        for s, c in enumerate(sent):
            c.wait_recv()
            v = v + dst[s]
        return v

    sent1 = across(swap1, part, from_core, mid, from_x, s3, r3)

    def from_pair(t, _):
        a_to(t * 2 + (1 - b), 0, pair).wait_recv()
        return 0

    lax.fori_loop(0, line, from_pair, 0)
    slot_a = owner[:, panel:] * wide_a + rank[:, panel:]

    def gather_a(i, acc):
        hi, lo = halves(got_a[i])
        p = onehot(slot_a == count((wide_a, panel), 0) + (i * wide_a).astype(F32))
        return acc + (dot(hi, p) + dot(lo, p))

    aq = lax.fori_loop(0, n_wide, gather_a, jnp.zeros((blocks, panel), F32))
    sent2 = across(swap2, part2, from_core2, mid2, from_x2, s4, r4)

    upd = total(sent1, part, from_core, from_x)
    w_one = a_one[...] - upd[:, :tile]
    wall[n, :, :tile] = w_one
    crossed = couple(aq - upd[:, tile:], *inv[0], 0)
    wall[n, :, tile:] = crossed

    spread = [rc(wall.at[n], wall.at[n], s5.at[s], r5.at[n], nar(chip_at(s), core)) for s in range(chips - 1)]
    for c in spread:
        c.start()
    twin = [rc(wall.at[n], wall.at[n], s6.at[0], r6.at[n], nar(x, 1 - core))]
    twin[0].start()
    l_one[...] = couple(w_one, *inv[0], 0)
    w_two = a_two[...] - total(sent2, part2, from_core2, from_x2)

    for s in range(chips - 1):
        item = chip_at(s) * 2 + core
        rc(wall.at[item], wall.at[item], s5.at[s], r5.at[item], nar(x, 1 - core)).wait_recv()
        c = rc(wall.at[item], wall.at[item], s6.at[s + 1], r6.at[item], nar(x, 1 - core))
        c.start()
        twin.append(c)
    for s in range(chips):
        item = chip_at(s) * 2 + (1 - core)
        rc(wall.at[item], wall.at[item], s6.at[s], r6.at[item], nar(x, 1 - core)).wait_recv()

    turned[...] = jnp.transpose(wall[:, :, tile:].reshape(panel, panel))
    ph, plo = halves(turned[pl.ds(pl.multiple_of(n * blocks, blocks), blocks), :])
    wh, wl = halves(wall[:, :, :tile].reshape(panel, tile))
    w_two = w_two - dot3(ph, plo, wh, wl)
    l_two[...] = couple(w_two, *inv[1], 0)

    for c in swap1 + swap2 + sent1 + sent2 + spread + twin:
        c.wait_send()
    for q in range(pieces):
        @pl.when(w != q)
        def _():
            post(q).wait_send()

    def drain(t, _):
        item = t * 2 + b
        for make, size in ((a_to, line), (piece_to, held)):
            @pl.when(t < size)
            def _():
                make(item, 2, pair).wait_send()

            @pl.when((t < size) & (t <= a) & has_right)
            def _():
                make(item, 0, pair).wait_send()

            @pl.when((t < size) & (t >= a) & has_left)
            def _():
                make(item, 1, pair).wait_send()

        return 0

    lax.fori_loop(0, line, drain, 0)


def shards(
    n_wide, n_narrow,
    prior_lt, prior_d, prior_e, prior_pairs, pivots, a_first, a_second, inv_d, inv_e, panel_pairs,
):
    k_local, tile = prior_lt.shape
    blocks = a_first.shape[0]
    panel = blocks * n_narrow
    cap = max(4 * panel // n_wide, 2)
    wide_a = -(-cap // 128) * 128
    line, chips = n_wide // 2, n_narrow // 2
    pieces = min(n_wide, k_local // 128)
    kk = k_local // pieces
    dma = pltpu.SemaphoreType.DMA
    vm = pltpu.VMEM
    ext = tile + panel
    out = jax.ShapeDtypeStruct((blocks, tile), F32)
    return pl.pallas_call(
        functools.partial(kernel, n_wide, n_narrow, cap, pieces),
        out_shape=(out, out),
        in_specs=[pl.BlockSpec(memory_space=pl.ANY)] + [pl.BlockSpec(memory_space=vm)] * 9,
        out_specs=(pl.BlockSpec(memory_space=vm),) * 2,
        scratch_shapes=[
            vm((k_local, tile), F32),
            vm((pieces, cap, kk), F32),
            vm((n_wide, cap, kk), F32),
            vm((pieces, 2 * panel, kk), F32),
            vm((n_wide, blocks, wide_a), F32),
            vm((2 * panel, n_wide * cap), BF16),
            vm((pieces, 8, kk), F32),
            vm((k_local, tile), BF16),
            vm((k_local, tile), BF16),
            vm((n_narrow, blocks, ext), F32),
            vm((n_narrow, blocks, tile), F32),
            vm((chips, blocks, ext), F32),
            vm((chips, blocks, tile), F32),
            vm((chips, blocks, ext), F32),
            vm((chips, blocks, tile), F32),
            vm((chips, blocks, ext), F32),
            vm((chips, blocks, tile), F32),
            vm((n_narrow, blocks, ext), F32),
            vm((panel, panel), F32),
            dma((pieces,)), dma((pieces,)), dma((n_wide,)),
            dma((line,)), dma((line,)), dma((line,)), dma((pieces,)),
            dma((line,)), dma((line,)), dma((line,)), dma((n_wide,)),
            dma((chips,)), dma((chips,)), dma((chips,)), dma((chips,)),
            dma((chips,)), dma((chips,)), dma((chips,)), dma((chips,)),
            dma((chips,)), dma((n_narrow,)), dma((chips,)), dma((n_narrow,)),
        ],
        compiler_params=pltpu.CompilerParams(
            collective_id=0, has_side_effects=True, vmem_limit_bytes=60 * 1024 * 1024
        ),
    )(
        prior_lt, prior_d[None, :], prior_e[None, :], prior_pairs[None, :], pivots,
        a_first, a_second, inv_d, inv_e, panel_pairs,
    )


def solution(mesh):
    in_specs = (
        P("narrow", "wide"),
        P("narrow"),
        P("narrow"),
        P("narrow"),
        P(),
        P("narrow", "wide"),
        P("narrow", "wide"),
        P(None, "narrow"),
        P(None, "narrow"),
        P(None, "narrow"),
    )
    out_specs = (P("narrow", "wide"), P("narrow", "wide"))
    body = functools.partial(shards, mesh.shape["wide"], mesh.shape["narrow"])
    return jax.shard_map(body, mesh=mesh, in_specs=in_specs, out_specs=out_specs, check_vma=False)
```

```python
import functools

import jax
import jax.numpy as jnp
from jax import lax
from jax.experimental import pallas as pl
from jax.experimental.pallas import tpu as pltpu
from jax.sharding import PartitionSpec as P

F32 = jnp.float32
BF16 = jnp.bfloat16
NN = (((1,), (0,)), ((), ()))
NT = (((1,), (1,)), ((), ()))


def dot(a, b, dims=NN):
    return lax.dot_general(a, b, dims, preferred_element_type=F32)


def halves(x):
    hi = x.astype(BF16)
    return hi, (x - hi.astype(F32)).astype(BF16)


def dot3(ahi, alo, bhi, blo, dims=NN):
    return dot(ahi, bhi, dims) + (dot(ahi, blo, dims) + dot(alo, bhi, dims))


def beside(block, joined, axis):
    return joined * pltpu.roll(block, block.shape[axis] - 1, axis) + pltpu.roll(joined * block, 1, axis)


def couple(block, diag, joined, axis):
    return diag * block + beside(block, joined, axis)


def count(shape, axis):
    return lax.broadcasted_iota(jnp.int32, shape, axis).astype(F32)


def column(row):
    size = row.shape[1]
    step = min(size, 128)
    eye = count((step, step), 0) == count((step, step), 1)
    return jnp.concatenate(
        [jnp.sum(jnp.where(eye, row[:, i:i + step], 0.0), axis=1, keepdims=True) for i in range(0, size, step)], 0
    )


def onehot(mask):
    return jnp.where(mask, 1.0, 0.0).astype(BF16)


def kernel(
    n_wide, n_narrow, cap, pieces,
    prior_hbm, diag, off, pairs, pivots, a_one, a_two, inv_d, inv_e, panel_pairs,
    l_one, l_two, side_one, side_two,
    prior, packed, inbox, dense, put, put_a, coef, dhi, dlo, part, part2, from_core, from_core2, mid, mid2,
    from_x, from_x2, wall, turned,
    s_load, s_post, r_post,
    s_right, s_left, s_pair, recv,
    s1, r1, s2, r2, s3, r3, s4, r4, s5, r5, s6, r6,
):
    k_local, tile = prior.shape
    blocks = a_one.shape[0]
    panel = blocks * n_narrow
    kk = k_local // pieces
    line = n_wide // 2
    held = pieces // 2
    chips = n_narrow // 2
    rows_a = blocks // pieces
    strips = panel // kk
    w = lax.axis_index("wide")
    n = lax.axis_index("narrow")
    a, b = w // 2, w % 2
    x, core = n // 2, n % 2
    pair = a * 2 + (1 - b)
    has_left, has_right = a > 0, a < line - 1
    mesh_ids = pl.DeviceIdType.MESH

    loads = [
        pltpu.make_async_copy(prior_hbm.at[pl.ds(q * kk, kk)], prior.at[pl.ds(q * kk, kk)], s_load.at[q])
        for q in range(pieces)
    ]
    for c in loads:
        c.start()

    barrier = pltpu.get_barrier_semaphore()

    def greet(to, which):
        pl.semaphore_signal(barrier, inc=1, device_id={"wide": to, "narrow": which}, device_id_type=mesh_ids)

    def greet_wide(i, _):
        greet(lax.rem(w + i, n_wide), n)
        return 0

    lax.fori_loop(1, n_wide, greet_wide, 0)

    def nar(cx, cc):
        return {"wide": w, "narrow": cx * 2 + cc}

    greet(w, x * 2 + (1 - core))
    for step in range(1, chips):
        greet(w, lax.rem(x + step, chips) * 2 + core)

    flat = jnp.concatenate([pivots[0:1, :], pivots[1:2, :]], 1).astype(F32)
    owner = jnp.floor((flat + 0.5) * (1.0 / tile))
    square = (2 * panel, 2 * panel)
    same = (column(owner) == owner) & (count(square, 0) < count(square, 1))
    rank = jnp.sum(jnp.where(same, 1.0, 0.0), axis=0, keepdims=True)
    here = w.astype(F32)
    hit = (owner == here) & (rank == count((kk, 2 * panel), 0))
    loc = jnp.sum(jnp.where(hit, flat - here * tile + 1.0, 0.0), axis=1, keepdims=True) - 1.0
    pick_a = onehot(loc == count((kk, tile), 1))
    pick = pick_a[:cap]

    pl.semaphore_wait(barrier, n_wide - 1 + chips)

    def post(q):
        return pltpu.make_async_remote_copy(
            src_ref=packed.at[q], dst_ref=inbox.at[w], send_sem=s_post.at[q], recv_sem=r_post.at[w],
            device_id={"wide": q, "narrow": n}, device_id_type=mesh_ids,
        )

    hi, lo = halves(a_one[...])
    packed_a = dot(hi, pick_a, NT) + dot(lo, pick_a, NT)
    for q in range(pieces):
        packed[q, cap:, :] = packed_a[q * rows_a:(q + 1) * rows_a, :]
    for q in range(pieces):
        loads[q].wait()
        hi, lo = halves(prior[q * kk:(q + 1) * kk, :])
        packed[q, :cap, :] = dot(pick, hi, NT) + dot(pick, lo, NT)

        @pl.when(w != q)
        def _():
            post(q).start()

    def move(buf, item, send, sem_at, rsem, to):
        return pltpu.make_async_remote_copy(
            src_ref=buf.at[item], dst_ref=buf.at[item], send_sem=send.at[sem_at], recv_sem=rsem.at[item],
            device_id={"wide": to, "narrow": n}, device_id_type=mesh_ids,
        )

    def piece_to(item, which, to):
        return move(dense, item, (s_right, s_left, s_pair)[which], item // 2, recv, to)

    def send_own(make):
        @pl.when(has_right)
        def _():
            make(w, 0, w + 2).start()

        @pl.when(has_left)
        def _():
            make(w, 1, w - 2).start()

        make(w, 2, pair).start()

    slots = n_wide * cap
    put[...] = onehot(column(owner * cap + rank) == count((2 * panel, slots), 1))
    joined = off[...] * pairs[...].astype(F32)
    for q in range(pieces):
        sl = slice(q * kk, (q + 1) * kk)
        coef[q, 0:1, :] = diag[:, sl]
        coef[q, 1:2, :] = joined[:, sl]

    slot_a = owner[:, panel:] * kk + rank[:, panel:]
    put_a[...] = onehot(slot_a == count((n_wide * kk, panel), 0))

    for q in range(pieces):
        sl = slice(q * kk, (q + 1) * kk)
        m = couple(prior[sl, :], column(diag[:, sl]), column(joined[:, sl]), 0)
        hi, lo = halves(m)
        dhi[sl, :] = hi
        dlo[sl, :] = lo
    part[...] = jnp.zeros_like(part)
    part2[...] = jnp.zeros_like(part2)

    inv_j = inv_e[...] * panel_pairs[...].astype(F32)
    inv = [(column(inv_d[i:i + 1, :]), column(inv_j[i:i + 1, :])) for i in range(2)]

    @pl.when(w < pieces)
    def _():
        inbox[w] = packed[w]

        def arrived(j, _):
            @pl.when(j != w)
            def _():
                pltpu.make_async_remote_copy(
                    src_ref=packed.at[0], dst_ref=inbox.at[j], send_sem=s_post.at[0], recv_sem=r_post.at[j],
                    device_id={"wide": pair, "narrow": n}, device_id_type=mesh_ids,
                ).wait_recv()

            return 0

        lax.fori_loop(0, n_wide, arrived, 0)
        hi, lo = halves(inbox[:, :cap, :].reshape(slots, kk))
        dense[w, :2 * panel, :] = dot(put[...], hi) + dot(put[...], lo)
        hi, lo = halves(jnp.concatenate([inbox[j, cap:, :] for j in range(n_wide)], 1))
        ordered = dot(hi, put_a[...]) + dot(lo, put_a[...])
        for i in range(strips):
            dense[w, 2 * panel + i * rows_a:2 * panel + (i + 1) * rows_a, :] = ordered[:, i * kk:(i + 1) * kk]
        send_own(piece_to)

    def fold(v):
        return v.reshape(n_narrow, blocks, v.shape[-1])

    def add_pair(p):
        c = [dense[2 * p + i, :2 * panel, :] for i in range(2)]
        e = [
            halves(couple(c[i][panel:], coef[2 * p + i, 0:1, :], coef[2 * p + i, 1:2, :], 1)) for i in range(2)
        ]
        c = [halves(v) for v in c]
        ch, cl = (jnp.concatenate([c[0][i], c[1][i]], 1) for i in range(2))
        eh, el = (jnp.concatenate([e[0][i], e[1][i]], 1) for i in range(2))
        rows = pl.ds(pl.multiple_of(p * 2 * kk, 2 * kk), 2 * kk)
        part[:, :, tile:] += fold(dot3(ch[:panel], cl[:panel], eh, el, NT))
        for j in range(0, tile, 256):
            cs = slice(j, j + 256)
            ph, pq = dhi[rows, cs], dlo[rows, cs]
            part[:, :, cs] += fold(dot3(ch[:panel], cl[:panel], ph, pq))
            part2[:, :, cs] += fold(dot3(ch[panel:], cl[panel:], ph, pq))

    def relay_item(make, item, ahead, which, to):
        make(item, 0, pair).wait_recv()
        make(item, 2, pair).start()

        @pl.when(ahead)
        def _():
            make(item, which, to).start()

    def step(t, _):
        @pl.when((t < line) & (a - t >= 0) & (a - t < held))
        def _():
            relay_item(piece_to, w - 2 * t, has_right, 0, w + 2)

        @pl.when((t < line) & (a + t < held))
        def _():
            relay_item(piece_to, w + 2 * t, has_left, 1, w - 2)

        def pair_at(p):
            piece_to(2 * p + (1 - b), 0, pair).wait_recv()
            add_pair(p)

        @pl.when((a - t + 1 >= 0) & (a - t + 1 < held))
        def _():
            pair_at(a - t + 1)

        @pl.when((t > 1) & (a + t - 1 < held))
        def _():
            pair_at(a + t - 1)

        return 0

    lax.fori_loop(1, line + 1, step, 0)

    def rc(src, dst, ss, rs, to):
        return pltpu.make_async_remote_copy(
            src_ref=src, dst_ref=dst, send_sem=ss, recv_sem=rs, device_id=to, device_id_type=pl.DeviceIdType.MESH,
        )

    def chip_at(s):
        return lax.rem(x + 1 + s, chips)

    def core_swap(src, dst, ss, rs):
        return [
            rc(src.at[chip_at(s) * 2 + (1 - core)], dst.at[s], ss.at[s], rs.at[s], nar(x, 1 - core))
            for s in range(chips)
        ]

    swap1 = core_swap(part, from_core, s1, r1)
    for c in swap1:
        c.start()
    swap2 = core_swap(part2, from_core2, s2, r2)
    for c in swap2:
        c.start()

    def across(swap, src, partner, middle, dst, ss, rs):
        out = []
        for s in range(chips - 1):
            swap[s].wait_recv()
            middle[s] = src[chip_at(s) * 2 + core] + partner[s]
            c = rc(middle.at[s], dst.at[s], ss.at[s], rs.at[s], nar(chip_at(s), core))
            c.start()
            out.append(c)
        swap[chips - 1].wait_recv()
        return out

    def total(sent, src, partner, dst):
        v = src[n] + partner[chips - 1]
        for s, c in enumerate(sent):
            c.wait_recv()
            v = v + dst[s]
        return v

    sent1 = across(swap1, part, from_core, mid, from_x, s3, r3)

    aq = jnp.concatenate(
        [dense[:, 2 * panel + i * rows_a:2 * panel + (i + 1) * rows_a, :].reshape(blocks, kk) for i in range(strips)], 1
    )
    sent2 = across(swap2, part2, from_core2, mid2, from_x2, s4, r4)

    upd = total(sent1, part, from_core, from_x)
    w_one = a_one[...] - upd[:, :tile]
    wall[n, :, :tile] = w_one
    crossed = couple(aq - upd[:, tile:], *inv[0], 0)
    wall[n, :, tile:] = crossed

    spread = [rc(wall.at[n], wall.at[n], s5.at[s], r5.at[n], nar(chip_at(s), core)) for s in range(chips - 1)]
    for c in spread:
        c.start()
    twin = [rc(wall.at[n], wall.at[n], s6.at[0], r6.at[n], nar(x, 1 - core))]
    twin[0].start()
    l_one[...] = w_one
    side_one[...] = beside(w_one, inv[0][1], 0)
    w_two = a_two[...] - total(sent2, part2, from_core2, from_x2)

    for s in range(chips - 1):
        item = chip_at(s) * 2 + core
        rc(wall.at[item], wall.at[item], s5.at[s], r5.at[item], nar(x, 1 - core)).wait_recv()
        c = rc(wall.at[item], wall.at[item], s6.at[s + 1], r6.at[item], nar(x, 1 - core))
        c.start()
        twin.append(c)
    for s in range(chips):
        item = chip_at(s) * 2 + (1 - core)
        rc(wall.at[item], wall.at[item], s6.at[s], r6.at[item], nar(x, 1 - core)).wait_recv()

    turned[...] = jnp.transpose(wall[:, :, tile:].reshape(panel, panel))
    ph, plo = halves(turned[pl.ds(pl.multiple_of(n * blocks, blocks), blocks), :])
    wh, wl = halves(wall[:, :, :tile].reshape(panel, tile))
    w_two = w_two - dot3(ph, plo, wh, wl)
    l_two[...] = w_two
    side_two[...] = beside(w_two, inv[1][1], 0)

    for c in swap1 + swap2 + sent1 + sent2 + spread + twin:
        c.wait_send()
    for q in range(pieces):
        @pl.when(w != q)
        def _():
            post(q).wait_send()

    def drain(t, _):
        item = t * 2 + b
        piece_to(item, 2, pair).wait_send()

        @pl.when((t <= a) & has_right)
        def _():
            piece_to(item, 0, pair).wait_send()

        @pl.when((t >= a) & has_left)
        def _():
            piece_to(item, 1, pair).wait_send()

        return 0

    lax.fori_loop(0, held, drain, 0)


def shards(
    n_wide, n_narrow,
    prior_lt, prior_d, prior_e, prior_pairs, pivots, a_first, a_second, inv_d, inv_e, panel_pairs,
):
    k_local, tile = prior_lt.shape
    blocks = a_first.shape[0]
    panel = blocks * n_narrow
    cap = max(4 * panel // n_wide, 2)
    line, chips = n_wide // 2, n_narrow // 2
    pieces = min(n_wide, k_local // 128)
    kk = k_local // pieces
    rows_a, strips = blocks // pieces, panel // kk
    dma = pltpu.SemaphoreType.DMA
    vm = pltpu.VMEM
    ext = tile + panel
    out = jax.ShapeDtypeStruct((blocks, tile), F32)
    w_one, w_two, side_one, side_two = pl.pallas_call(
        functools.partial(kernel, n_wide, n_narrow, cap, pieces),
        out_shape=(out,) * 4,
        in_specs=[pl.BlockSpec(memory_space=pl.ANY)] + [pl.BlockSpec(memory_space=vm)] * 9,
        out_specs=(pl.BlockSpec(memory_space=vm),) * 4,
        scratch_shapes=[
            vm((k_local, tile), F32),
            vm((pieces, cap + rows_a, kk), F32),
            vm((n_wide, cap + rows_a, kk), F32),
            vm((pieces, 2 * panel + strips * rows_a, kk), F32),
            vm((2 * panel, n_wide * cap), BF16),
            vm((n_wide * kk, panel), BF16),
            vm((pieces, 8, kk), F32),
            vm((k_local, tile), BF16),
            vm((k_local, tile), BF16),
            vm((n_narrow, blocks, ext), F32),
            vm((n_narrow, blocks, tile), F32),
            vm((chips, blocks, ext), F32),
            vm((chips, blocks, tile), F32),
            vm((chips, blocks, ext), F32),
            vm((chips, blocks, tile), F32),
            vm((chips, blocks, ext), F32),
            vm((chips, blocks, tile), F32),
            vm((n_narrow, blocks, ext), F32),
            vm((panel, panel), F32),
            dma((pieces,)), dma((pieces,)), dma((n_wide,)),
            dma((line,)), dma((line,)), dma((line,)), dma((pieces,)),
            dma((chips,)), dma((chips,)), dma((chips,)), dma((chips,)),
            dma((chips,)), dma((chips,)), dma((chips,)), dma((chips,)),
            dma((chips,)), dma((n_narrow,)), dma((chips,)), dma((n_narrow,)),
        ],
        compiler_params=pltpu.CompilerParams(
            collective_id=0, has_side_effects=True, vmem_limit_bytes=60 * 1024 * 1024
        ),
    )(
        prior_lt, prior_d[None, :], prior_e[None, :], prior_pairs[None, :], pivots,
        a_first, a_second, inv_d, inv_e, panel_pairs,
    )
    return inv_d[0][:, None] * w_one + side_one, inv_d[1][:, None] * w_two + side_two


def solution(mesh):
    in_specs = (
        P("narrow", "wide"),
        P("narrow"),
        P("narrow"),
        P("narrow"),
        P(),
        P("narrow", "wide"),
        P("narrow", "wide"),
        P(None, "narrow"),
        P(None, "narrow"),
        P(None, "narrow"),
    )
    out_specs = (P("narrow", "wide"), P("narrow", "wide"))
    body = functools.partial(shards, mesh.shape["wide"], mesh.shape["narrow"])
    return jax.shard_map(body, mesh=mesh, in_specs=in_specs, out_specs=out_specs, check_vma=False)
```

```python
import functools

import jax
import jax.numpy as jnp
from jax import lax
from jax.experimental import pallas as pl
from jax.experimental.pallas import tpu as pltpu
from jax.sharding import PartitionSpec as P

F32 = jnp.float32
BF16 = jnp.bfloat16
NN = (((1,), (0,)), ((), ()))
NT = (((1,), (1,)), ((), ()))


def dot(a, b, dims=NN):
    return lax.dot_general(a, b, dims, preferred_element_type=F32)


def halves(x):
    hi = x.astype(BF16)
    return hi, (x - hi.astype(F32)).astype(BF16)


def dot3(ahi, alo, bhi, blo, dims=NN):
    return dot(ahi, bhi, dims) + (dot(ahi, blo, dims) + dot(alo, bhi, dims))


def beside(block, joined, axis):
    return joined * pltpu.roll(block, block.shape[axis] - 1, axis) + pltpu.roll(joined * block, 1, axis)


def couple(block, diag, joined, axis):
    return diag * block + beside(block, joined, axis)


def count(shape, axis):
    return lax.broadcasted_iota(jnp.int32, shape, axis).astype(F32)


def column(row):
    size = row.shape[1]
    step = min(size, 128)
    eye = count((step, step), 0) == count((step, step), 1)
    return jnp.concatenate(
        [jnp.sum(jnp.where(eye, row[:, i:i + step], 0.0), axis=1, keepdims=True) for i in range(0, size, step)], 0
    )


def onehot(mask):
    return jnp.where(mask, 1.0, 0.0).astype(BF16)


def kernel(
    n_wide, n_narrow, cap, pieces,
    prior_hbm, diag, off, pairs, pivots, a_one, a_two, inv_d, inv_e, panel_pairs,
    l_one, l_two, side_one, side_two,
    prior, packed, inbox, dense, put, put_a, coef, dhi, dlo, part, part2, from_core, from_core2, mid, mid2,
    from_x, from_x2, wall, turned,
    s_load, s_post, r_post,
    s_right, s_left, s_pair, recv,
    s1, r1, s2, r2, s3, r3, s4, r4, s5, r5, s6, r6,
):
    k_local, tile = prior.shape
    blocks = a_one.shape[0]
    panel = blocks * n_narrow
    kk = k_local // pieces
    line = n_wide // 2
    held = pieces // 2
    chips = n_narrow // 2
    rows_a = blocks // pieces
    strips = panel // kk
    w = lax.axis_index("wide")
    n = lax.axis_index("narrow")
    a, b = w // 2, w % 2
    x, core = n // 2, n % 2
    pair = a * 2 + (1 - b)
    has_left, has_right = a > 0, a < line - 1
    mesh_ids = pl.DeviceIdType.MESH

    loads = [
        pltpu.make_async_copy(prior_hbm.at[pl.ds(q * kk, kk)], prior.at[pl.ds(q * kk, kk)], s_load.at[q])
        for q in range(pieces)
    ]
    for c in loads:
        c.start()

    barrier = pltpu.get_barrier_semaphore()

    def greet(to, which):
        pl.semaphore_signal(barrier, inc=1, device_id={"wide": to, "narrow": which}, device_id_type=mesh_ids)

    def greet_wide(i, _):
        greet(lax.rem(w + i, n_wide), n)
        return 0

    lax.fori_loop(1, n_wide, greet_wide, 0)

    def nar(cx, cc):
        return {"wide": w, "narrow": cx * 2 + cc}

    greet(w, x * 2 + (1 - core))
    for step in range(1, chips):
        greet(w, lax.rem(x + step, chips) * 2 + core)

    flat = jnp.concatenate([pivots[0:1, :], pivots[1:2, :]], 1).astype(F32)
    owner = jnp.floor((flat + 0.5) * (1.0 / tile))
    square = (2 * panel, 2 * panel)
    same = (column(owner) == owner) & (count(square, 0) < count(square, 1))
    rank = jnp.sum(jnp.where(same, 1.0, 0.0), axis=0, keepdims=True)
    here = w.astype(F32)
    hit = (owner == here) & (rank == count((kk, 2 * panel), 0))
    loc = jnp.sum(jnp.where(hit, flat - here * tile + 1.0, 0.0), axis=1, keepdims=True) - 1.0
    pick_a = onehot(loc == count((kk, tile), 1))
    pick = pick_a[:cap]

    pl.semaphore_wait(barrier, n_wide - 1 + chips)

    def post(q):
        return pltpu.make_async_remote_copy(
            src_ref=packed.at[q], dst_ref=inbox.at[w], send_sem=s_post.at[q], recv_sem=r_post.at[w],
            device_id={"wide": q, "narrow": n}, device_id_type=mesh_ids,
        )

    hi, lo = halves(a_one[...])
    packed_a = dot(hi, pick_a, NT) + dot(lo, pick_a, NT)
    for q in range(pieces):
        packed[q, cap:, :] = packed_a[q * rows_a:(q + 1) * rows_a, :]
    for q in range(pieces):
        loads[q].wait()
        hi, lo = halves(prior[q * kk:(q + 1) * kk, :])
        packed[q, :cap, :] = dot(pick, hi, NT) + dot(pick, lo, NT)

        @pl.when(w != q)
        def _():
            post(q).start()

    half = dense.shape[1] // 2

    def piece_to(item, which, to, h):
        at = dense.at[item, pl.ds(h * half, half)]
        return pltpu.make_async_remote_copy(
            src_ref=at, dst_ref=at, send_sem=(s_right, s_left, s_pair)[which].at[item // 2, h],
            recv_sem=recv.at[item, h], device_id={"wide": to, "narrow": n}, device_id_type=mesh_ids,
        )

    def send_own():
        for h in range(2):
            @pl.when(has_right)
            def _():
                piece_to(w, 0, w + 2, h).start()

            @pl.when(has_left)
            def _():
                piece_to(w, 1, w - 2, h).start()

            piece_to(w, 2, pair, h).start()

    slots = n_wide * cap
    put[...] = onehot(column(owner * cap + rank) == count((2 * panel, slots), 1))
    joined = off[...] * pairs[...].astype(F32)
    for q in range(pieces):
        sl = slice(q * kk, (q + 1) * kk)
        coef[q, 0:1, :] = diag[:, sl]
        coef[q, 1:2, :] = joined[:, sl]

    slot_a = owner[:, panel:] * kk + rank[:, panel:]
    put_a[...] = onehot(slot_a == count((n_wide * kk, panel), 0))

    for q in range(pieces):
        sl = slice(q * kk, (q + 1) * kk)
        m = couple(prior[sl, :], column(diag[:, sl]), column(joined[:, sl]), 0)
        hi, lo = halves(m)
        dhi[sl, :] = hi
        dlo[sl, :] = lo
    part[...] = jnp.zeros_like(part)
    part2[...] = jnp.zeros_like(part2)

    inv_j = inv_e[...] * panel_pairs[...].astype(F32)
    inv = [(column(inv_d[i:i + 1, :]), column(inv_j[i:i + 1, :])) for i in range(2)]

    @pl.when(w < pieces)
    def _():
        inbox[w] = packed[w]

        def arrived(j, _):
            @pl.when(j != w)
            def _():
                pltpu.make_async_remote_copy(
                    src_ref=packed.at[0], dst_ref=inbox.at[j], send_sem=s_post.at[0], recv_sem=r_post.at[j],
                    device_id={"wide": pair, "narrow": n}, device_id_type=mesh_ids,
                ).wait_recv()

            return 0

        lax.fori_loop(0, n_wide, arrived, 0)
        hi, lo = halves(inbox[:, :cap, :].reshape(slots, kk))
        dense[w, :2 * panel, :] = dot(put[...], hi) + dot(put[...], lo)
        hi, lo = halves(jnp.concatenate([inbox[j, cap:, :] for j in range(n_wide)], 1))
        ordered = dot(hi, put_a[...]) + dot(lo, put_a[...])
        for i in range(strips):
            dense[w, 2 * panel + i * rows_a:2 * panel + (i + 1) * rows_a, :] = ordered[:, i * kk:(i + 1) * kk]
        send_own()

    def fold(v):
        return v.reshape(n_narrow, blocks, v.shape[-1])

    def add_pair(p):
        c = [dense[2 * p + i, :2 * panel, :] for i in range(2)]
        e = [
            halves(couple(c[i][panel:], coef[2 * p + i, 0:1, :], coef[2 * p + i, 1:2, :], 1)) for i in range(2)
        ]
        c = [halves(v) for v in c]
        ch, cl = (jnp.concatenate([c[0][i], c[1][i]], 1) for i in range(2))
        eh, el = (jnp.concatenate([e[0][i], e[1][i]], 1) for i in range(2))
        rows = pl.ds(pl.multiple_of(p * 2 * kk, 2 * kk), 2 * kk)
        part[:, :, tile:] += fold(dot3(ch[:panel], cl[:panel], eh, el, NT))
        for j in range(0, tile, 256):
            cs = slice(j, j + 256)
            ph, pq = dhi[rows, cs], dlo[rows, cs]
            part[:, :, cs] += fold(dot3(ch[:panel], cl[:panel], ph, pq))
            part2[:, :, cs] += fold(dot3(ch[panel:], cl[panel:], ph, pq))

    def relay_item(item, ahead, which, to, h):
        piece_to(item, 0, pair, h).wait_recv()

        @pl.when(ahead)
        def _():
            piece_to(item, which, to, h).start()

        piece_to(item, 2, pair, h).start()

    def step(t, _):
        for h in range(2):
            @pl.when((t < line) & (a - t >= 0) & (a - t < held))
            def _():
                relay_item(w - 2 * t, has_right, 0, w + 2, h)

            @pl.when((t < line) & (a + t < held))
            def _():
                relay_item(w + 2 * t, has_left, 1, w - 2, h)

        def pair_at(p):
            for h in range(2):
                piece_to(2 * p + (1 - b), 0, pair, h).wait_recv()
            add_pair(p)

        @pl.when((a - t + 1 >= 0) & (a - t + 1 < held))
        def _():
            pair_at(a - t + 1)

        @pl.when((t > 1) & (a + t - 1 < held))
        def _():
            pair_at(a + t - 1)

        return 0

    lax.fori_loop(1, line + 1, step, 0)

    def rc(src, dst, ss, rs, to):
        return pltpu.make_async_remote_copy(
            src_ref=src, dst_ref=dst, send_sem=ss, recv_sem=rs, device_id=to, device_id_type=pl.DeviceIdType.MESH,
        )

    def chip_at(s):
        return lax.rem(x + 1 + s, chips)

    def core_swap(src, dst, ss, rs):
        return [
            rc(src.at[chip_at(s) * 2 + (1 - core)], dst.at[s], ss.at[s], rs.at[s], nar(x, 1 - core))
            for s in range(chips)
        ]

    swap1 = core_swap(part, from_core, s1, r1)
    for c in swap1:
        c.start()
    swap2 = core_swap(part2, from_core2, s2, r2)
    for c in swap2:
        c.start()

    def across(swap, src, partner, middle, dst, ss, rs):
        out = []
        for s in range(chips - 1):
            swap[s].wait_recv()
            middle[s] = src[chip_at(s) * 2 + core] + partner[s]
            c = rc(middle.at[s], dst.at[s], ss.at[s], rs.at[s], nar(chip_at(s), core))
            c.start()
            out.append(c)
        swap[chips - 1].wait_recv()
        return out

    def total(sent, src, partner, dst):
        v = src[n] + partner[chips - 1]
        for s, c in enumerate(sent):
            c.wait_recv()
            v = v + dst[s]
        return v

    sent1 = across(swap1, part, from_core, mid, from_x, s3, r3)

    aq = jnp.concatenate(
        [dense[:, 2 * panel + i * rows_a:2 * panel + (i + 1) * rows_a, :].reshape(blocks, kk) for i in range(strips)], 1
    )
    sent2 = across(swap2, part2, from_core2, mid2, from_x2, s4, r4)

    upd = total(sent1, part, from_core, from_x)
    w_one = a_one[...] - upd[:, :tile]
    wall[n, :, :tile] = w_one
    crossed = couple(aq - upd[:, tile:], *inv[0], 0)
    wall[n, :, tile:] = crossed

    spread = [rc(wall.at[n], wall.at[n], s5.at[s], r5.at[n], nar(chip_at(s), core)) for s in range(chips - 1)]
    for c in spread:
        c.start()
    twin = [rc(wall.at[n], wall.at[n], s6.at[0], r6.at[n], nar(x, 1 - core))]
    twin[0].start()
    l_one[...] = w_one
    side_one[...] = beside(w_one, inv[0][1], 0)
    w_two = a_two[...] - total(sent2, part2, from_core2, from_x2)

    for s in range(chips - 1):
        item = chip_at(s) * 2 + core
        rc(wall.at[item], wall.at[item], s5.at[s], r5.at[item], nar(x, 1 - core)).wait_recv()
        c = rc(wall.at[item], wall.at[item], s6.at[s + 1], r6.at[item], nar(x, 1 - core))
        c.start()
        twin.append(c)
    for s in range(chips):
        item = chip_at(s) * 2 + (1 - core)
        rc(wall.at[item], wall.at[item], s6.at[s], r6.at[item], nar(x, 1 - core)).wait_recv()

    turned[...] = jnp.transpose(wall[:, :, tile:].reshape(panel, panel))
    ph, plo = halves(turned[pl.ds(pl.multiple_of(n * blocks, blocks), blocks), :])
    wh, wl = halves(wall[:, :, :tile].reshape(panel, tile))
    w_two = w_two - dot3(ph, plo, wh, wl)
    l_two[...] = w_two
    side_two[...] = beside(w_two, inv[1][1], 0)

    for c in swap1 + swap2 + sent1 + sent2 + spread + twin:
        c.wait_send()
    for q in range(pieces):
        @pl.when(w != q)
        def _():
            post(q).wait_send()

    def drain(t, _):
        item = t * 2 + b
        for h in range(2):
            piece_to(item, 2, pair, h).wait_send()

            @pl.when((t <= a) & has_right)
            def _():
                piece_to(item, 0, pair, h).wait_send()

            @pl.when((t >= a) & has_left)
            def _():
                piece_to(item, 1, pair, h).wait_send()

        return 0

    lax.fori_loop(0, held, drain, 0)


def shards(
    n_wide, n_narrow,
    prior_lt, prior_d, prior_e, prior_pairs, pivots, a_first, a_second, inv_d, inv_e, panel_pairs,
):
    k_local, tile = prior_lt.shape
    blocks = a_first.shape[0]
    panel = blocks * n_narrow
    cap = max(4 * panel // n_wide, 2)
    line, chips = n_wide // 2, n_narrow // 2
    pieces = min(n_wide, k_local // 128)
    kk = k_local // pieces
    rows_a, strips = blocks // pieces, panel // kk
    dma = pltpu.SemaphoreType.DMA
    vm = pltpu.VMEM
    ext = tile + panel
    out = jax.ShapeDtypeStruct((blocks, tile), F32)
    w_one, w_two, side_one, side_two = pl.pallas_call(
        functools.partial(kernel, n_wide, n_narrow, cap, pieces),
        out_shape=(out,) * 4,
        in_specs=[pl.BlockSpec(memory_space=pl.ANY)] + [pl.BlockSpec(memory_space=vm)] * 9,
        out_specs=(pl.BlockSpec(memory_space=vm),) * 4,
        scratch_shapes=[
            vm((k_local, tile), F32),
            vm((pieces, cap + rows_a, kk), F32),
            vm((n_wide, cap + rows_a, kk), F32),
            vm((pieces, 2 * panel + strips * rows_a, kk), F32),
            vm((2 * panel, n_wide * cap), BF16),
            vm((n_wide * kk, panel), BF16),
            vm((pieces, 8, kk), F32),
            vm((k_local, tile), BF16),
            vm((k_local, tile), BF16),
            vm((n_narrow, blocks, ext), F32),
            vm((n_narrow, blocks, tile), F32),
            vm((chips, blocks, ext), F32),
            vm((chips, blocks, tile), F32),
            vm((chips, blocks, ext), F32),
            vm((chips, blocks, tile), F32),
            vm((chips, blocks, ext), F32),
            vm((chips, blocks, tile), F32),
            vm((n_narrow, blocks, ext), F32),
            vm((panel, panel), F32),
            dma((pieces,)), dma((pieces,)), dma((n_wide,)),
            dma((line, 2)), dma((line, 2)), dma((line, 2)), dma((pieces, 2)),
            dma((chips,)), dma((chips,)), dma((chips,)), dma((chips,)),
            dma((chips,)), dma((chips,)), dma((chips,)), dma((chips,)),
            dma((chips,)), dma((n_narrow,)), dma((chips,)), dma((n_narrow,)),
        ],
        compiler_params=pltpu.CompilerParams(
            collective_id=0, has_side_effects=True, vmem_limit_bytes=60 * 1024 * 1024
        ),
    )(
        prior_lt, prior_d[None, :], prior_e[None, :], prior_pairs[None, :], pivots,
        a_first, a_second, inv_d, inv_e, panel_pairs,
    )
    return inv_d[0][:, None] * w_one + side_one, inv_d[1][:, None] * w_two + side_two


def solution(mesh):
    in_specs = (
        P("narrow", "wide"),
        P("narrow"),
        P("narrow"),
        P("narrow"),
        P(),
        P("narrow", "wide"),
        P("narrow", "wide"),
        P(None, "narrow"),
        P(None, "narrow"),
        P(None, "narrow"),
    )
    out_specs = (P("narrow", "wide"), P("narrow", "wide"))
    body = functools.partial(shards, mesh.shape["wide"], mesh.shape["narrow"])
    return jax.shard_map(body, mesh=mesh, in_specs=in_specs, out_specs=out_specs, check_vma=False)
```
